32 devices in a mesh: groups: 2 (over x), tok: 16 (over z, y, core).
Axes of the slice: x: 2, y: 2, z: 4, core: 2. Of those that a mesh axis runs over, the one named last changes fastest.
Arguments:
- tokens: bfloat16 [8192, 1024], P(('groups', 'tok')), parts along dimension 0, may hold values from -6 to 6
- norm_gain: float32 [1024], replicated, may hold values from 0.1 to 1.9
- w_qk: bfloat16 [1024, 1024], replicated, may hold values from -0.1875 to 0.1875
- w_v: bfloat16 [1024, 1024], replicated, may hold values from -0.1875 to 0.1875
- cotangent: bfloat16 [8192, 1024], P(('groups', 'tok')), parts along dimension 0, may hold values from -48 to 48
- log_sums: float32 [2, 8, 8192], P(None, None, ('groups', 'tok')), parts along dimension 2, may hold values from 7 to 8
- bucket_order: int32 [2, 8192], P(None, 'groups'), parts along dimension 1, may hold values from 0 to 4095, as said below
- token_position: int32 [2, 8192], P(None, ('groups', 'tok')), parts along dimension 1, may hold values from 0 to 4095, as said below
Outputs:
- d_tokens: bfloat16 [8192, 1024], P(('groups', 'tok')), parts along dimension 0
- d_gain: float32 [2048], P(('groups', 'tok')), parts along dimension 0
- d_wqk: float32 [2048, 1024], P(('groups', 'tok')), parts along dimension 0
- d_wv: float32 [2048, 1024], P(('groups', 'tok')), parts along dimension 0
The draws below stay inside these ranges and needn't reach their ends.
There are 2 independent parts, one for each index of `groups`. The reference program is written for one: setup_inputs(seed, part) draws one part's arguments, and reference() takes and returns one part's arrays. A program takes and returns all parts, laid end to end along the dimension named above; an argument that names none is the same for every part. Nothing has to cross between parts.
Inputs may be any that keep to these rules, and one draw needn't show every extreme that they name: `bucket_order`: each row is a permutation; the 256 hash-sorted positions of one device hold at most 20 tokens of any one device's 256 tokens, and exactly 20 of at least one. token_position[r, bucket_order[r, p]] = p.
All inputs are finite; a program needn't handle non-finite values.
Results may differ from the reference program's by a relative error of at most 0.025.
Values may be sent and summed in bfloat16 or wider, within the bound.
A program may use at most 128 MiB of HBM per device.

```python
import math
import jax
import jax.numpy as jnp
from jax import lax

H = 8
DH = 128
D = 1024
BLOCK = 256
ROUNDS = 2
TOK_DEV = 256
TOKENS = 4096
CAP = 20
N_TOK = 16


def build_orderings(key):
    orderings = []
    for hashing in range(ROUNDS):
        round_key = jax.random.fold_in(key, 7001 + hashing)
        device_key, jitter_key, source_key, target_key, tie_key = jax.random.split(round_key, 5)
        spare_rows = TOK_DEV - CAP
        base_load = spare_rows // (N_TOK - 1)
        extra_rows = spare_rows % (N_TOK - 1)
        placed = jax.random.permutation(device_key, N_TOK).astype(jnp.int32)
        jitter = jax.random.randint(jitter_key, (N_TOK - 1,), 0, base_load // 4 + 1).astype(jnp.int32)
        weights = base_load + (jnp.arange(N_TOK - 1) < extra_rows).astype(jnp.int32) + jitter - jnp.roll(jitter, -1)
        weights = jnp.concatenate([jnp.array([CAP], jnp.int32), weights.astype(jnp.int32)])
        source_ids = jnp.broadcast_to(jnp.arange(N_TOK, dtype=jnp.int32)[:, None], (N_TOK, N_TOK))
        offsets = jnp.broadcast_to(jnp.arange(N_TOK, dtype=jnp.int32)[None, :], (N_TOK, N_TOK))
        target = placed[(source_ids + offsets) % N_TOK]
        pair_loads = jnp.zeros((N_TOK, N_TOK), jnp.int32).at[source_ids, target].set(jnp.broadcast_to(weights[None, :], (N_TOK, N_TOK)))

        def spread(row_load, subkey):
            listed = jnp.repeat(jnp.arange(N_TOK, dtype=jnp.int32), row_load, total_repeat_length=TOK_DEV)
            return jax.random.permutation(subkey, listed)
        token_dest = jax.vmap(spread)(pair_loads, jax.random.split(source_key, N_TOK)).reshape(-1).astype(jnp.int32)
        slot_source = jax.vmap(spread)(pair_loads.T, jax.random.split(target_key, N_TOK)).reshape(-1).astype(jnp.int32)
        tiebreak = jax.random.permutation(tie_key, TOKENS).astype(jnp.int32)
        block_ids = (jnp.arange(TOKENS, dtype=jnp.int32) // TOK_DEV).astype(jnp.int32)
        token_score = (token_dest * N_TOK + block_ids) * TOKENS + tiebreak
        place_score = (block_ids * N_TOK + slot_source) * TOKENS + jnp.arange(TOKENS, dtype=jnp.int32)
        token_sorted = jnp.argsort(token_score, stable=True).astype(jnp.int32)
        place_sorted = jnp.argsort(place_score, stable=True).astype(jnp.int32)
        ordering = jnp.zeros((TOKENS,), jnp.int32).at[place_sorted].set(token_sorted)
        orderings.append(ordering)
    return jnp.stack(orderings)


def draw_bucket_order(key, part):
    return build_orderings(key)


def draw_token_position(key, part):
    orderings = build_orderings(key)
    places = jnp.arange(TOKENS, dtype=jnp.int32)
    return jnp.stack([jnp.zeros((TOKENS,), jnp.int32).at[orderings[hashing]].set(places) for hashing in range(ROUNDS)])


def spiked(drawn, stream_key, source, target, blocks, factor):
    owner, partner = [(jnp.arange(drawn.shape[position]) // (drawn.shape[position] // blocks)).reshape([-1 if axis == position else 1 for axis in range(drawn.ndim)]) for position in (source, target)]
    chosen = jax.random.permutation(stream_key, blocks)[partner]
    strong = (owner == chosen) | (owner == (partner + blocks // 2) % blocks)
    return jnp.where(strong, factor * drawn, drawn)


def shard_levels(rng, extent, cuts, least, largest):
    factor_of = 1.0
    for dim, parts in cuts:
        steps = jax.random.uniform(jax.random.fold_in(jax.random.fold_in(rng, 6), dim), (parts,), jnp.float32, least / len(cuts), largest / len(cuts))
        factor_of = factor_of * jnp.repeat(jnp.exp(steps), extent[dim] // parts).reshape((-1,) + (1,) * (len(extent) - 1 - dim))
    return factor_of


def scatter_about(key, shape, width, reach, cuts=(), held_as=jnp.bfloat16):
    values = jax.random.normal(key, shape, jnp.float32) * width
    if len(cuts) > 0:
        values = shard_levels(key, shape, cuts, -0.22, 0.18) * values
    return jnp.clip(values, min=-reach, max=reach).astype(held_as)


def noise_with(own_key, shape, deviation, reach, cuts, heavy, held_as=jnp.bfloat16):
    drawn = deviation * jax.random.normal(own_key, shape, jnp.float32)
    if cuts:
        drawn = drawn * shard_levels(own_key, shape, cuts, -0.22, 0.18)
    return jnp.clip(spiked(drawn, jax.random.fold_in(own_key, 3), *heavy), -reach, reach).astype(held_as)


def setup_inputs(seed: int = 0, part: int = 0) -> dict:
    key_of = jax.random.split(jax.random.key(seed), 9)
    own_keys = jax.random.split(jax.random.fold_in(key_of[8], part), 9)
    return {
        "tokens": noise_with(own_keys[0], (TOKENS, D), 1.0, 6.0, ((0, 16),), (0, 1, 16, 2.0)),
        "norm_gain": jnp.clip(1.0 + 0.18 * jax.random.normal(key_of[1], (D,), jnp.float32), 0.1, 1.9),
        "w_qk": scatter_about(key_of[2], (D, D), D ** -0.5, 0.1875),
        "w_v": scatter_about(key_of[3], (D, D), D ** -0.5, 0.1875),
        "cotangent": scatter_about(own_keys[4], (TOKENS, D), 8.0, 48.0, ((0, 16),)),
        "log_sums": jnp.clip(7.0 + 1.0 * jax.random.uniform(own_keys[5], (ROUNDS, H, TOKENS), jnp.float32) ** shard_levels(own_keys[5], (ROUNDS, H, TOKENS), ((2, 16),), -0.2, 0.2), 7.0, 8.0),
        "bucket_order": draw_bucket_order(jax.random.fold_in(jax.random.fold_in(key_of[8], part), 71), part),
        "token_position": draw_token_position(jax.random.fold_in(jax.random.fold_in(key_of[8], part), 71), part),
    }


def normed(values, scales):
    return values * lax.rsqrt(lax.optimization_barrier(jnp.mean(values * values, axis=-1, keepdims=True)) + 1e-06) * scales

def unit_keys(queries):
    head_depth = queries.shape[-1]
    return queries * lax.rsqrt(lax.optimization_barrier(jnp.mean(queries * queries, axis=-1, keepdims=True)) + 1e-06) / math.sqrt(head_depth)

def attend(queries, keys_all, values_all, out_grads, log_sum):
    block_len = queries.shape[1]
    queries_f = queries.astype(jnp.float32)
    keys_f = keys_all.astype(jnp.float32)
    values_f = values_all.astype(jnp.float32)
    grads_f = out_grads.astype(jnp.float32)
    scores = jnp.einsum('cihe,cjhe->chij', queries_f, keys_f)
    diagonal = jnp.arange(2 * block_len)[None, :] == jnp.arange(block_len)[:, None] + block_len
    weights = jnp.where(diagonal, 0.0, jnp.exp(scores - log_sum[:, :, :, None]))
    d_weights = jnp.einsum('cihe,cjhe->chij', grads_f, values_f)
    totals = lax.optimization_barrier(jnp.sum(weights * d_weights, axis=-1, keepdims=True))
    d_scores = (weights * (d_weights - totals)).astype(jnp.bfloat16).astype(jnp.float32)
    weights_low = weights.astype(jnp.bfloat16).astype(jnp.float32)
    d_values = jnp.einsum('chij,cihe->cjhe', weights_low, grads_f)
    d_queries = jnp.einsum('chij,cjhe->cihe', d_scores, keys_f)
    d_keys = jnp.einsum('chij,cihe->cjhe', d_scores, queries_f)
    return (d_queries, d_keys, d_values)

def one_block(members):
    results = attend(*[member[None] for member in members])
    return tuple((result[0] for result in results))

def reference(tokens, norm_gain, w_qk, w_v, cotangent, log_sums, bucket_order, token_position):
    tokens_wide = tokens.astype(jnp.float32)
    normal_rows = normed(tokens_wide, norm_gain).astype(jnp.bfloat16)
    query_rows = jnp.dot(normal_rows, w_qk, preferred_element_type=jnp.float32).astype(jnp.bfloat16)
    value_rows = jnp.dot(normal_rows, w_v, preferred_element_type=jnp.float32).astype(jnp.bfloat16)
    block_count = TOKENS // BLOCK
    d_normal = jnp.zeros((TOKENS, D), jnp.float32)
    grad_qk = jnp.zeros((D, D), jnp.float32)
    grad_v = jnp.zeros((D, D), jnp.float32)
    for hashing in range(ROUNDS):
        order_row = bucket_order[hashing]
        query_four = query_rows[order_row].reshape(block_count, BLOCK, H, DH)
        value_four = value_rows[order_row].reshape(block_count, BLOCK, H, DH)
        grad_four = cotangent[order_row].reshape(block_count, BLOCK, H, DH)
        unit_four = unit_keys(query_four.astype(jnp.float32)).astype(jnp.bfloat16)
        block_sums = log_sums[hashing].reshape(H, block_count, BLOCK).transpose(1, 0, 2)
        keys_all = jnp.concatenate([jnp.roll(unit_four, 1, axis=0), unit_four], axis=1)
        values_all = jnp.concatenate([jnp.roll(value_four, 1, axis=0), value_four], axis=1)
        d_query, d_keys, d_values = lax.map(one_block, (query_four, keys_all, values_all, grad_four, block_sums))
        key_grad = d_keys[:, BLOCK:] + jnp.roll(d_keys[:, :BLOCK], -1, axis=0)
        value_grad = d_values[:, BLOCK:] + jnp.roll(d_values[:, :BLOCK], -1, axis=0)
        _, key_pull = jax.vjp(unit_keys, query_four.astype(jnp.float32))
        query_grad = d_query + key_pull(key_grad)[0]
        places = token_position[hashing]
        query_low = query_grad.reshape(TOKENS, D).astype(jnp.bfloat16)[places]
        value_low = value_grad.reshape(TOKENS, D).astype(jnp.bfloat16)[places]
        grad_qk = grad_qk + jnp.dot(normal_rows.T, query_low, preferred_element_type=jnp.float32)
        grad_v = grad_v + jnp.dot(normal_rows.T, value_low, preferred_element_type=jnp.float32)
        d_normal = d_normal + jnp.dot(query_low, w_qk.T, preferred_element_type=jnp.float32) + jnp.dot(value_low, w_v.T, preferred_element_type=jnp.float32)
    _, norm_pull = jax.vjp(normed, tokens_wide, norm_gain)
    d_tokens, grad_gain = norm_pull(d_normal)
    grad_scale = 1.0 / math.sqrt(TOKENS)
    return (d_tokens.astype(jnp.bfloat16), grad_gain * grad_scale, grad_qk * grad_scale, grad_v * grad_scale)
```

```python
import functools
import math

import jax
import jax.numpy as jnp
from jax import lax
from jax.experimental import pallas as pl
from jax.experimental.pallas import tpu as pltpu
from jax.sharding import PartitionSpec as P

BLOCK = 256
EPS = 1e-06
VMEM_LIMIT = 60 * 1024 * 1024
MESH = pl.DeviceIdType.MESH
F32 = jnp.float32
BF16 = jnp.bfloat16


def whole(count):
    return [pl.BlockSpec(memory_space=pltpu.VMEM)] * count


def dot_nn(a, b):
    return lax.dot_general(a, b, (((1,), (0,)), ((), ())), preferred_element_type=F32)


def dot_nt(a, b):
    return lax.dot_general(a, b, (((1,), (1,)), ((), ())), preferred_element_type=F32)


def dot_tn(a, b):
    return lax.dot_general(a, b, (((0,), (0,)), ((), ())), preferred_element_type=F32)


def params(**more):
    return pltpu.CompilerParams(vmem_limit_bytes=VMEM_LIMIT, **more)


def slot_row(groups, order, stride, cap_offset):
    size = groups.shape[1]
    groups_col = jnp.broadcast_to(groups, (size, size)).T
    order_col = jnp.broadcast_to(order, (size, size)).T
    earlier = (groups_col == groups) & (order_col < order)
    rank = jnp.sum(earlier.astype(F32), axis=0, keepdims=True).astype(jnp.int32)
    return groups * stride + rank + cap_offset


def one_hot_rows(slots, slot_count):
    size = slots.shape[1]
    ids = lax.broadcasted_iota(jnp.int32, (slot_count, size), 0)
    return jnp.where(ids == slots, 1.0, 0.0).astype(BF16)


def home_slots(places, tok_dev, stride, cap_offset):
    return slot_row(lax.div(places, jnp.int32(tok_dev)), places, stride, cap_offset)


def sorted_slots(order, tok_dev, stride, cap_offset):
    position = lax.broadcasted_iota(jnp.int32, order.shape, 1)
    return slot_row(lax.div(order, jnp.int32(tok_dev)), position, stride, cap_offset)


def dispatch_kernel(devices, capacity, chunk, places_ref, tokens_ref, cot_ref, out_ref):
    rounds, tok_dev = places_ref.shape
    for hashing in range(rounds):
        places = places_ref[hashing : hashing + 1, :]
        slots = home_slots(places, tok_dev, chunk, 0)
        rows = dot_nn(one_hot_rows(slots, devices * chunk), tokens_ref[...])
        rows += dot_nn(one_hot_rows(slots + capacity, devices * chunk), cot_ref[...])
        out_ref[hashing] = rows.astype(BF16)


def exchange_kernel(pieces, *refs):
    sources, targets = refs[:pieces], refs[pieces : 2 * pieces]
    send_sem, recv_sem, own_sem = refs[2 * pieces :]
    devices = lax.axis_size("tok")
    me = lax.axis_index("tok")
    barrier = pltpu.get_barrier_semaphore()
    for step in range(1, devices):
        peer = lax.rem(me + step, devices)
        pl.semaphore_signal(barrier, inc=1, device_id={"tok": peer}, device_id_type=MESH)
    own = [
        pltpu.make_async_copy(sources[i].at[me], targets[i].at[me], own_sem.at[i])
        for i in range(pieces)
    ]
    for copy in own:
        copy.start()
    pl.semaphore_wait(barrier, devices - 1)
    copies = []
    for i in range(pieces):
        for step in range(1, devices):
            peer = lax.rem(me + step, devices)
            copy = pltpu.make_async_remote_copy(
                src_ref=sources[i].at[peer],
                dst_ref=targets[i].at[me],
                send_sem=send_sem.at[i, step - 1],
                recv_sem=recv_sem.at[i, step - 1],
                device_id={"tok": peer},
                device_id_type=MESH,
            )
            copy.start()
            copies.append(copy)
    for copy in own:
        copy.wait()
    for copy in copies:
        copy.wait()


def exchange(arrays, collective_id):
    devices = lax.axis_size("tok")
    pieces = len(arrays)
    return pl.pallas_call(
        functools.partial(exchange_kernel, pieces),
        out_shape=[jax.ShapeDtypeStruct(a.shape, a.dtype) for a in arrays],
        in_specs=[pl.BlockSpec(memory_space=pl.ANY)] * pieces,
        out_specs=[pl.BlockSpec(memory_space=pl.ANY)] * pieces,
        scratch_shapes=[
            pltpu.SemaphoreType.DMA((pieces, devices - 1)),
            pltpu.SemaphoreType.DMA((pieces, devices - 1)),
            pltpu.SemaphoreType.DMA((pieces,)),
        ],
        compiler_params=pltpu.CompilerParams(collective_id=collective_id, has_side_effects=True),
    )(*arrays)


def sort_kernel(capacity, chunk, order_ref, arrived_ref, x_ref, g_ref):
    tok_dev = order_ref.shape[2]
    slot_count = arrived_ref.shape[1]
    slots = sorted_slots(order_ref[0], tok_dev, chunk, 0)
    rows = arrived_ref[0]
    x_ref[0] = dot_tn(one_hot_rows(slots, slot_count), rows).astype(BF16)
    g_ref[0] = dot_tn(one_hot_rows(slots + capacity, slot_count), rows).astype(BF16)


def normal_of(x, gain):
    return (x * lax.rsqrt(jnp.mean(x * x, axis=-1, keepdims=True) + EPS) * gain).astype(BF16)


def unit_of(q):
    depth = q.shape[-1]
    scale = lax.rsqrt(jnp.mean(q * q, axis=-1, keepdims=True) + EPS)
    return (q * scale / math.sqrt(depth)).astype(BF16)


def project_kernel(x_ref, gain_ref, qk_ref, v_ref, normal_ref, query_ref, value_ref):
    normal = normal_of(x_ref[0].astype(F32), gain_ref[...])
    normal_ref[0] = normal
    query_ref[0] = dot_nn(normal, qk_ref[...]).astype(BF16)
    value_ref[0] = dot_nn(normal, v_ref[...]).astype(BF16)


def attend_kernel(
    halo_ref, gain_ref, qk_ref, v_ref, query_ref, value_ref, g_ref, sums_ref,
    dq_ref, dk_ref, dv_ref, back_ref, halo_q, halo_v,
):
    heads = sums_ref.shape[1]
    rows, width = query_ref.shape[1:]
    depth = width // heads
    normal = normal_of(halo_ref[0].astype(F32), gain_ref[...])
    halo_q[...] = dot_nn(normal, qk_ref[...]).astype(BF16)
    halo_v[...] = dot_nn(normal, v_ref[...]).astype(BF16)
    sums = sums_ref[0].T
    diagonal = lax.broadcasted_iota(jnp.int32, (rows, rows), 0) == lax.broadcasted_iota(
        jnp.int32, (rows, rows), 1
    )
    for head in range(heads):
        part = slice(head * depth, (head + 1) * depth)
        query = query_ref[0, :, part]
        g = g_ref[0, :, part]
        log_sum = sums[:, head : head + 1]
        keys = [unit_of(halo_q[:, part].astype(F32)), unit_of(query.astype(F32))]
        values = [halo_v[:, part], value_ref[0, :, part]]
        weights = [jnp.exp(dot_nt(query, k) - log_sum) for k in keys]
        weights[1] = jnp.where(diagonal, 0.0, weights[1])
        d_weights = [dot_nt(g, v) for v in values]
        total = jnp.sum(weights[0] * d_weights[0] + weights[1] * d_weights[1], -1, keepdims=True)
        d_scores = [(w * (d - total)).astype(BF16) for w, d in zip(weights, d_weights)]
        low = [w.astype(BF16) for w in weights]
        dq_ref[0, :, part] = dot_nn(d_scores[0], keys[0]) + dot_nn(d_scores[1], keys[1])
        dk_ref[0, :, part] = dot_tn(d_scores[1], query)
        dv_ref[0, :, part] = dot_tn(low[1], g)
        back_ref[0, :, part] = dot_tn(d_scores[0], query).astype(BF16)
        back_ref[0, :, width + head * depth : width + (head + 1) * depth] = dot_tn(
            low[0], g
        ).astype(BF16)


def finish_kernel(
    heads, devices, capacity, chunk, grad_scale,
    order_ref, x_ref, normal_ref, query_ref, dq_ref, dk_ref, dv_ref, back_ref, qk_ref, v_ref,
    weights_ref, out_ref, gain_ref, query_low, value_low, rows_low,
):
    rounds, rows, width = query_ref.shape
    depth = width // heads
    gain = jnp.zeros((1, width), F32)
    for hashing in range(rounds):
        span = slice(hashing * rows, (hashing + 1) * rows)
        for head in range(heads):
            part = slice(head * depth, (head + 1) * depth)
            q = query_ref[hashing, :, part].astype(F32)
            dk = dk_ref[hashing, :, part] + back_ref[hashing, :, part].astype(F32)
            scale = lax.rsqrt(jnp.mean(q * q, axis=-1, keepdims=True) + EPS)
            along = jnp.mean(q * dk, axis=-1, keepdims=True)
            pulled = (dk * scale - q * (scale * scale * scale * along)) / math.sqrt(depth)
            query_low[span, part] = (dq_ref[hashing, :, part] + pulled).astype(BF16)
        value_low[span, :] = (
            dv_ref[hashing] + back_ref[hashing, :, width:].astype(F32)
        ).astype(BF16)
        d_normal = dot_nt(query_low[span, :], qk_ref[...]) + dot_nt(value_low[span, :], v_ref[...])
        x = x_ref[hashing].astype(F32)
        scaled = x * lax.rsqrt(jnp.mean(x * x, axis=-1, keepdims=True) + EPS)
        gain += jnp.sum(d_normal * scaled, axis=0, keepdims=True)
        rows_low[span, :] = d_normal.astype(BF16)
    gain_ref[...] = gain * grad_scale
    normal = normal_ref[...].reshape(rounds * rows, width)
    weights_ref[:, :width] = (dot_tn(normal, query_low[...]) * grad_scale).astype(BF16)
    weights_ref[:, width:] = (dot_tn(normal, value_low[...]) * grad_scale).astype(BF16)
    out = jnp.zeros((devices * chunk, width), F32)
    for hashing in range(rounds):
        slots = sorted_slots(order_ref[hashing], rows, chunk, hashing * capacity)
        out += dot_nn(
            one_hot_rows(slots, devices * chunk), rows_low[hashing * rows : (hashing + 1) * rows, :]
        )
    out_ref[...] = out.astype(BF16)


def home_kernel(capacity, chunk, places_ref, back_ref, tokens_ref, gain_ref, parts_ref, out_ref, total_ref):
    rounds, tok_dev = places_ref.shape
    slot_count = back_ref.shape[0]
    picks = None
    for hashing in range(rounds):
        slots = home_slots(places_ref[hashing : hashing + 1, :], tok_dev, chunk, hashing * capacity)
        ones = one_hot_rows(slots, slot_count)
        picks = ones if picks is None else picks + ones
    d_normal = dot_tn(picks, back_ref[...])
    x = tokens_ref[...].astype(F32)
    scale = lax.rsqrt(jnp.mean(x * x, axis=-1, keepdims=True) + EPS)
    t = d_normal * gain_ref[...]
    along = jnp.mean(x * t, axis=-1, keepdims=True)
    out_ref[...] = (t * scale - x * (scale * scale * scale * along)).astype(BF16)
    total_ref[...] = jnp.sum(parts_ref[:, 0, :], axis=0, keepdims=True)


def per_device(tokens, norm_gain, w_qk, w_v, cotangent, log_sums, bucket_order, token_position):
    devices = lax.axis_size("tok")
    me = lax.axis_index("tok")
    tok_dev, width = tokens.shape
    rounds, seq_len = bucket_order.shape
    heads = log_sums.shape[1]
    assert tok_dev == BLOCK
    capacity = 5 * tok_dev // (4 * devices)
    kinds = max(2, rounds)
    chunk = -(-kinds * capacity // 8) * 8
    slots = devices * chunk
    grad_scale = 1.0 / math.sqrt(seq_len)
    gain_row = norm_gain.reshape(1, width)
    my_order = lax.dynamic_slice_in_dim(bucket_order, me * tok_dev, tok_dev, axis=1).reshape(
        rounds, 1, tok_dev
    )
    round_rows = jax.ShapeDtypeStruct((rounds, tok_dev, width), BF16)
    round_rows_f = jax.ShapeDtypeStruct((rounds, tok_dev, width), F32)

    def per_round(*shape):
        return pl.BlockSpec((1,) + shape, lambda r: (r, 0, 0))

    def shared(*shape):
        return pl.BlockSpec(shape, lambda r: (0, 0))

    row_spec = per_round(tok_dev, width)

    outbound = pl.pallas_call(
        functools.partial(dispatch_kernel, devices, capacity, chunk),
        out_shape=jax.ShapeDtypeStruct((rounds, slots, width), BF16),
        in_specs=whole(3),
        out_specs=whole(1)[0],
        compiler_params=params(),
        name="dispatch",
    )(token_position, tokens, cotangent)
    arrived = exchange(
        [outbound[r].reshape(devices, chunk, width) for r in range(rounds)], collective_id=0
    )
    arrived = jnp.stack([a.reshape(slots, width) for a in arrived])
    sorted_x, sorted_g = pl.pallas_call(
        functools.partial(sort_kernel, capacity, chunk),
        grid=(rounds,),
        out_shape=[round_rows, round_rows],
        in_specs=[per_round(1, tok_dev), per_round(slots, width)],
        out_specs=[row_spec, row_spec],
        compiler_params=params(),
        name="sort",
    )(my_order, arrived)
    route = [(i, (i + 1) % devices) for i in range(devices)]
    halo_x = lax.ppermute(sorted_x, "tok", route)
    normal, query, value = pl.pallas_call(
        project_kernel,
        grid=(rounds,),
        out_shape=[round_rows] * 3,
        in_specs=[row_spec, shared(1, width), shared(width, width), shared(width, width)],
        out_specs=[row_spec] * 3,
        compiler_params=params(),
        name="project",
        cost_estimate=pl.CostEstimate(
            flops=4 * rounds * tok_dev * width * width,
            bytes_accessed=4 * width * width + 8 * rounds * tok_dev * width,
            transcendentals=0,
        ),
    )(sorted_x, gain_row, w_qk, w_v)
    dq, dk, dv, back = pl.pallas_call(
        attend_kernel,
        grid=(rounds,),
        out_shape=[round_rows_f] * 3
        + [jax.ShapeDtypeStruct((rounds, tok_dev, 2 * width), BF16)],
        in_specs=[
            row_spec, shared(1, width), shared(width, width), shared(width, width),
            row_spec, row_spec, row_spec, per_round(heads, tok_dev),
        ],
        out_specs=[row_spec] * 3 + [per_round(tok_dev, 2 * width)],
        scratch_shapes=[pltpu.VMEM((tok_dev, width), BF16)] * 2,
        compiler_params=params(),
        name="attend",
    )(halo_x, gain_row, w_qk, w_v, query, value, sorted_g, log_sums)
    returned = lax.ppermute(back, "tok", [(b, a) for a, b in route])
    weights, rows_out, gain_part = pl.pallas_call(
        functools.partial(finish_kernel, heads, devices, capacity, chunk, grad_scale),
        out_shape=[
            jax.ShapeDtypeStruct((width, 2 * width), BF16),
            jax.ShapeDtypeStruct((slots, width), BF16),
            jax.ShapeDtypeStruct((1, width), F32),
        ],
        in_specs=whole(10),
        out_specs=whole(3),
        scratch_shapes=[pltpu.VMEM((rounds * tok_dev, width), BF16)] * 3,
        compiler_params=params(),
        name="finish",
    )(my_order, sorted_x, normal, query, dq, dk, dv, returned, w_qk, w_v)
    grads = lax.psum_scatter(weights, "tok", scatter_dimension=0, tiled=True).astype(F32)
    own = width // devices
    gain_slices = jnp.pad(gain_part.reshape(devices, 1, own), ((0, 0), (0, 7), (0, 128 - own)))
    rows_back, gain_back = exchange(
        [rows_out.reshape(devices, chunk, width), gain_slices], collective_id=1
    )
    d_tokens, d_gain = pl.pallas_call(
        functools.partial(home_kernel, capacity, chunk),
        out_shape=[
            jax.ShapeDtypeStruct((tok_dev, width), BF16),
            jax.ShapeDtypeStruct((1, 128), F32),
        ],
        in_specs=whole(5),
        out_specs=whole(2),
        compiler_params=params(),
        name="home",
    )(token_position, rows_back.reshape(slots, width), tokens, gain_row, gain_back)
    return (d_tokens, d_gain[0, :own], grads[:, :width], grads[:, width:])


def solution(mesh):
    in_specs = (
        P(("groups", "tok"), None),
        P(),
        P(),
        P(),
        P(("groups", "tok"), None),
        P(None, None, ("groups", "tok")),
        P(None, "groups"),
        P(None, ("groups", "tok")),
    )
    out_specs = (
        P(("groups", "tok"), None),
        P(("groups", "tok")),
        P(("groups", "tok"), None),
        P(("groups", "tok"), None),
    )
    return jax.shard_map(
        per_device, mesh=mesh, in_specs=in_specs, out_specs=out_specs, check_vma=False
    )
```

```python
import functools
import math

import jax
import jax.numpy as jnp
from jax import lax
from jax.experimental import pallas as pl
from jax.experimental.pallas import tpu as pltpu
from jax.sharding import PartitionSpec as P

BLOCK = 256
EPS = 1e-06
VMEM_LIMIT = 60 * 1024 * 1024
MESH = pl.DeviceIdType.MESH
F32 = jnp.float32
BF16 = jnp.bfloat16


def whole(count):
    return [pl.BlockSpec(memory_space=pltpu.VMEM)] * count


def dot_nn(a, b):
    return lax.dot_general(a, b, (((1,), (0,)), ((), ())), preferred_element_type=F32)


def dot_nt(a, b):
    return lax.dot_general(a, b, (((1,), (1,)), ((), ())), preferred_element_type=F32)


def dot_tn(a, b):
    return lax.dot_general(a, b, (((0,), (0,)), ((), ())), preferred_element_type=F32)


def params(**more):
    return pltpu.CompilerParams(vmem_limit_bytes=VMEM_LIMIT, **more)


def slot_row(groups, order, stride, cap_offset):
    size = groups.shape[1]
    groups_col = jnp.broadcast_to(groups, (size, size)).T
    order_col = jnp.broadcast_to(order, (size, size)).T
    earlier = (groups_col == groups) & (order_col < order)
    rank = jnp.sum(earlier.astype(F32), axis=0, keepdims=True).astype(jnp.int32)
    return groups * stride + rank + cap_offset


def one_hot_rows(slots, slot_count):
    size = slots.shape[1]
    ids = lax.broadcasted_iota(jnp.int32, (slot_count, size), 0)
    return jnp.where(ids == slots, 1.0, 0.0).astype(BF16)


def home_slots(places, tok_dev, stride, cap_offset):
    return slot_row(lax.div(places, jnp.int32(tok_dev)), places, stride, cap_offset)


def sorted_slots(order, tok_dev, stride, cap_offset):
    position = lax.broadcasted_iota(jnp.int32, order.shape, 1)
    return slot_row(lax.div(order, jnp.int32(tok_dev)), position, stride, cap_offset)


def dispatch_kernel(devices, capacity, chunk, places_ref, tokens_ref, cot_ref, *out_refs):
    rounds, tok_dev = places_ref.shape
    for hashing in range(rounds):
        places = places_ref[hashing : hashing + 1, :]
        slots = home_slots(places, tok_dev, chunk, 0)
        rows = dot_nn(one_hot_rows(slots, devices * chunk), tokens_ref[...])
        rows += dot_nn(one_hot_rows(slots + capacity, devices * chunk), cot_ref[...])
        out_refs[hashing][...] = rows.astype(BF16)


def exchange_kernel(pieces, *refs):
    sources, targets = refs[:pieces], refs[pieces : 2 * pieces]
    send_sem, recv_sem, own_sem = refs[2 * pieces :]
    devices = lax.axis_size("tok")
    me = lax.axis_index("tok")
    barrier = pltpu.get_barrier_semaphore()
    for step in range(1, devices):
        peer = lax.rem(me + step, devices)
        pl.semaphore_signal(barrier, inc=1, device_id={"tok": peer}, device_id_type=MESH)
    own = [
        pltpu.make_async_copy(sources[i].at[me], targets[i].at[me], own_sem.at[i])
        for i in range(pieces)
    ]
    for copy in own:
        copy.start()
    pl.semaphore_wait(barrier, devices - 1)
    copies = []
    for i in range(pieces):
        for step in range(1, devices):
            peer = lax.rem(me + step, devices)
            copy = pltpu.make_async_remote_copy(
                src_ref=sources[i].at[peer],
                dst_ref=targets[i].at[me],
                send_sem=send_sem.at[i, step - 1],
                recv_sem=recv_sem.at[i, step - 1],
                device_id={"tok": peer},
                device_id_type=MESH,
            )
            copy.start()
            copies.append(copy)
    for copy in own:
        copy.wait()
    for copy in copies:
        copy.wait()


def exchange(arrays, collective_id):
    devices = lax.axis_size("tok")
    pieces = len(arrays)
    return pl.pallas_call(
        functools.partial(exchange_kernel, pieces),
        out_shape=[jax.ShapeDtypeStruct(a.shape, a.dtype) for a in arrays],
        in_specs=[pl.BlockSpec(memory_space=pl.ANY)] * pieces,
        out_specs=[pl.BlockSpec(memory_space=pl.ANY)] * pieces,
        scratch_shapes=[
            pltpu.SemaphoreType.DMA((pieces, devices - 1)),
            pltpu.SemaphoreType.DMA((pieces, devices - 1)),
            pltpu.SemaphoreType.DMA((pieces,)),
        ],
        compiler_params=pltpu.CompilerParams(collective_id=collective_id, has_side_effects=True),
    )(*arrays)


def normal_of(x, gain):
    return (x * lax.rsqrt(jnp.mean(x * x, axis=-1, keepdims=True) + EPS) * gain).astype(BF16)


def unit_of(q):
    depth = q.shape[-1]
    scale = lax.rsqrt(jnp.mean(q * q, axis=-1, keepdims=True) + EPS)
    return (q * scale / math.sqrt(depth)).astype(BF16)


def core_kernel(heads, capacity, chunk, ahead, grad_scale, *refs):
    rounds = refs[0].shape[0]
    order_ref, gain_ref, qk_ref, v_ref, sums_ref = refs[:5]
    outgoing = refs[5 : 5 + rounds]
    weights_ref, out_ref, gain_out = refs[5 + rounds : 8 + rounds]
    (
        arrived, sorted_x, sorted_g, halo_x, normal, query, value, halo_q, halo_v,
        d_query, d_key, d_value, back_out, back_in, query_low, value_low, rows_low, total,
        send_sem, recv_sem, own_sem, halo_sem, back_sem,
    ) = refs[8 + rounds :]
    devices = lax.axis_size("tok")
    me = lax.axis_index("tok")
    right, left = lax.rem(me + 1, devices), lax.rem(me + devices - 1, devices)
    rows, width = sorted_x.shape[1:]
    depth = width // heads
    slot_count = devices * chunk
    parts = [slice(head * depth, (head + 1) * depth) for head in range(heads)]

    barrier = pltpu.get_barrier_semaphore()
    for step in range(1, devices):
        peer = lax.rem(me + step, devices)
        pl.semaphore_signal(barrier, inc=1, device_id={"tok": peer}, device_id_type=MESH)
    own = [
        pltpu.make_async_copy(outgoing[r].at[me], arrived.at[r, me], own_sem.at[r])
        for r in range(rounds)
    ]
    for copy in own:
        copy.start()
    pl.semaphore_wait(barrier, devices - 1)

    def piece(r, step):
        peer = lax.rem(me + step, devices)
        return pltpu.make_async_remote_copy(
            src_ref=outgoing[r].at[peer],
            dst_ref=arrived.at[r, me],
            send_sem=send_sem.at[r, step - 1],
            recv_sem=recv_sem.at[r, step - 1],
            device_id={"tok": peer},
            device_id_type=MESH,
        )

    pieces = [[piece(r, step) for step in range(1, devices)] for r in range(rounds)]
    halos = [
        pltpu.make_async_remote_copy(
            src_ref=sorted_x.at[r],
            dst_ref=halo_x.at[r],
            send_sem=halo_sem.at[0, r],
            recv_sem=halo_sem.at[1, r],
            device_id={"tok": right},
            device_id_type=MESH,
        )
        for r in range(rounds)
    ]
    backs = [
        pltpu.make_async_remote_copy(
            src_ref=back_out.at[r],
            dst_ref=back_in.at[r],
            send_sem=back_sem.at[0, r],
            recv_sem=back_sem.at[1, r],
            device_id={"tok": left},
            device_id_type=MESH,
        )
        for r in range(rounds)
    ]
    for copy in pieces[0]:
        copy.start()

    def sort(r):
        slots = sorted_slots(order_ref[r], rows, chunk, 0)
        data = arrived[r].reshape(slot_count, width)
        sorted_x[r] = dot_tn(one_hot_rows(slots, slot_count), data).astype(BF16)
        sorted_g[r] = dot_tn(one_hot_rows(slots + capacity, slot_count), data).astype(BF16)

    def project(r):
        normal[r] = normal_of(sorted_x[r].astype(F32), gain_ref[...])
        query[r] = dot_nn(normal[r], qk_ref[...]).astype(BF16)
        value[r] = dot_nn(normal[r], v_ref[...]).astype(BF16)

    def attend(r):
        behind = normal_of(halo_x[r].astype(F32), gain_ref[...])
        halo_q[...] = dot_nn(behind, qk_ref[...]).astype(BF16)
        halo_v[...] = dot_nn(behind, v_ref[...]).astype(BF16)
        sums = sums_ref[r].T
        diagonal = lax.broadcasted_iota(jnp.int32, (rows, rows), 0) == lax.broadcasted_iota(
            jnp.int32, (rows, rows), 1
        )
        for head, part in enumerate(parts):
            q = query[r, :, part]
            g = sorted_g[r, :, part]
            log_sum = sums[:, head : head + 1]
            keys = [unit_of(halo_q[:, part].astype(F32)), unit_of(q.astype(F32))]
            values = [halo_v[:, part], value[r, :, part]]
            weights = [jnp.exp(dot_nt(q, k) - log_sum) for k in keys]
            weights[1] = jnp.where(diagonal, 0.0, weights[1])
            d_weights = [dot_nt(g, v) for v in values]
            delta = jnp.sum(
                weights[0] * d_weights[0] + weights[1] * d_weights[1], -1, keepdims=True
            )
            d_scores = [(w * (d - delta)).astype(BF16) for w, d in zip(weights, d_weights)]
            low = [w.astype(BF16) for w in weights]
            back_out[r, :, part] = dot_tn(d_scores[0], q).astype(BF16)
            back_out[r, :, slice(width + part.start, width + part.stop)] = dot_tn(
                low[0], g
            ).astype(BF16)
            d_query[r, :, part] = dot_nn(d_scores[0], keys[0]) + dot_nn(d_scores[1], keys[1])
            d_key[r, :, part] = dot_tn(d_scores[1], q)
            d_value[r, :, part] = dot_tn(low[1], g)

    def finish(r):
        for part in parts:
            q = query[r, :, part].astype(F32)
            dk = d_key[r, :, part] + back_in[r, :, part].astype(F32)
            scale = lax.rsqrt(jnp.mean(q * q, axis=-1, keepdims=True) + EPS)
            along = jnp.mean(q * dk, axis=-1, keepdims=True)
            pulled = (dk * scale - q * (scale * scale * scale * along)) / math.sqrt(depth)
            query_low[:, part] = (d_query[r, :, part] + pulled).astype(BF16)
        value_low[...] = (d_value[r] + back_in[r, :, width:].astype(F32)).astype(BF16)
        d_normal = dot_nt(query_low[...], qk_ref[...]) + dot_nt(value_low[...], v_ref[...])
        x = sorted_x[r].astype(F32)
        scaled = x * lax.rsqrt(jnp.mean(x * x, axis=-1, keepdims=True) + EPS)
        rows_low[r] = d_normal.astype(BF16)
        for low, columns in (
            (query_low, slice(0, width)),
            (value_low, slice(width, 2 * width)),
        ):
            grad = dot_tn(normal[r], low[...])
            if r > 0:
                grad += total[:, columns]
            if r < rounds - 1:
                total[:, columns] = grad
            else:
                weights_ref[:, columns] = (grad * grad_scale).astype(BF16)
        return jnp.sum(d_normal * scaled, axis=0, keepdims=True)

    for r in range(rounds):
        if r + 1 < rounds:
            for copy in pieces[r + 1][:ahead]:
                copy.start()
        own[r].wait()
        for copy in pieces[r]:
            copy.wait_recv()
        sort(r)
        halos[r].start()
        if r + 1 < rounds:
            for copy in pieces[r + 1][ahead:]:
                copy.start()
        project(r)
        halos[r].wait_recv()
        attend(r)
        backs[r].start()
    gain_total = jnp.zeros((1, width), F32)
    for r in range(rounds):
        backs[r].wait_recv()
        gain_total += finish(r)
    gain_total = gain_total * grad_scale
    share = width // devices
    gain_out[...] = jnp.zeros(gain_out.shape, F32)
    for device in range(devices):
        gain_out[device, 0:1, 0:share] = gain_total[:, device * share : (device + 1) * share]
    out = jnp.zeros((slot_count, width), F32)
    for r in range(rounds):
        slots = sorted_slots(order_ref[r], rows, chunk, r * capacity)
        out += dot_nn(one_hot_rows(slots, slot_count), rows_low[r])
    out_ref[...] = out.astype(BF16)
    for r in range(rounds):
        for copy in pieces[r]:
            copy.wait_send()
        halos[r].wait_send()
        backs[r].wait_send()


def home_kernel(capacity, chunk, places_ref, back_ref, tokens_ref, gain_ref, parts_ref, out_ref, total_ref):
    rounds, tok_dev = places_ref.shape
    slot_count = back_ref.shape[0]
    picks = None
    for hashing in range(rounds):
        slots = home_slots(places_ref[hashing : hashing + 1, :], tok_dev, chunk, hashing * capacity)
        ones = one_hot_rows(slots, slot_count)
        picks = ones if picks is None else picks + ones
    d_normal = dot_tn(picks, back_ref[...])
    x = tokens_ref[...].astype(F32)
    scale = lax.rsqrt(jnp.mean(x * x, axis=-1, keepdims=True) + EPS)
    t = d_normal * gain_ref[...]
    along = jnp.mean(x * t, axis=-1, keepdims=True)
    out_ref[...] = (t * scale - x * (scale * scale * scale * along)).astype(BF16)
    total_ref[...] = jnp.sum(parts_ref[:, 0, :], axis=0, keepdims=True)


def per_device(tokens, norm_gain, w_qk, w_v, cotangent, log_sums, bucket_order, token_position):
    devices = lax.axis_size("tok")
    me = lax.axis_index("tok")
    tok_dev, width = tokens.shape
    rounds, seq_len = bucket_order.shape
    heads = log_sums.shape[1]
    assert tok_dev == BLOCK
    capacity = 5 * tok_dev // (4 * devices)
    kinds = max(2, rounds)
    chunk = -(-kinds * capacity // 8) * 8
    slots = devices * chunk
    grad_scale = 1.0 / math.sqrt(seq_len)
    gain_row = norm_gain.reshape(1, width)
    my_order = lax.dynamic_slice_in_dim(bucket_order, me * tok_dev, tok_dev, axis=1).reshape(
        rounds, 1, tok_dev
    )
    outgoing = pl.pallas_call(
        functools.partial(dispatch_kernel, devices, capacity, chunk),
        out_shape=[jax.ShapeDtypeStruct((slots, width), BF16)] * rounds,
        in_specs=whole(3),
        out_specs=whole(rounds),
        compiler_params=params(),
        name="dispatch",
    )(token_position, tokens, cotangent)

    def low(*shape):
        return pltpu.VMEM(shape, BF16)

    per_round = (rounds, tok_dev, width)
    weights, rows_out, gain_slices = pl.pallas_call(
        functools.partial(core_kernel, heads, capacity, chunk, devices // 3, grad_scale),
        out_shape=[
            jax.ShapeDtypeStruct((width, 2 * width), BF16),
            jax.ShapeDtypeStruct((slots, width), BF16),
            jax.ShapeDtypeStruct((devices, 8, 128), F32),
        ],
        in_specs=whole(5) + [pl.BlockSpec(memory_space=pl.ANY)] * rounds,
        out_specs=whole(3),
        scratch_shapes=[
            low(rounds, devices, chunk, width),
            *[low(*per_round)] * 6,
            *[low(tok_dev, width)] * 2,
            *[pltpu.VMEM(per_round, F32)] * 3,
            *[low(rounds, tok_dev, 2 * width)] * 2,
            *[low(tok_dev, width)] * 2,
            low(*per_round),
            pltpu.VMEM((width, 2 * width), F32),
            pltpu.SemaphoreType.DMA((rounds, devices - 1)),
            pltpu.SemaphoreType.DMA((rounds, devices - 1)),
            pltpu.SemaphoreType.DMA((rounds,)),
            pltpu.SemaphoreType.DMA((2, rounds)),
            pltpu.SemaphoreType.DMA((2, rounds)),
        ],
        compiler_params=params(collective_id=0, has_side_effects=True),
        name="core",
    )(
        my_order, gain_row, w_qk, w_v, log_sums,
        *[rows.reshape(devices, chunk, width) for rows in outgoing],
    )
    grads = lax.psum_scatter(weights, "tok", scatter_dimension=0, tiled=True).astype(F32)
    own = width // devices
    rows_back, gain_back = exchange(
        [rows_out.reshape(devices, chunk, width), gain_slices], collective_id=1
    )
    d_tokens, d_gain = pl.pallas_call(
        functools.partial(home_kernel, capacity, chunk),
        out_shape=[
            jax.ShapeDtypeStruct((tok_dev, width), BF16),
            jax.ShapeDtypeStruct((1, 128), F32),
        ],
        in_specs=whole(5),
        out_specs=whole(2),
        compiler_params=params(),
        name="home",
    )(token_position, rows_back.reshape(slots, width), tokens, gain_row, gain_back)
    return (d_tokens, d_gain[0, :own], grads[:, :width], grads[:, width:])


def solution(mesh):
    in_specs = (
        P(("groups", "tok"), None),
        P(),
        P(),
        P(),
        P(("groups", "tok"), None),
        P(None, None, ("groups", "tok")),
        P(None, "groups"),
        P(None, ("groups", "tok")),
    )
    out_specs = (
        P(("groups", "tok"), None),
        P(("groups", "tok")),
        P(("groups", "tok"), None),
        P(("groups", "tok"), None),
    )
    return jax.shard_map(
        per_device, mesh=mesh, in_specs=in_specs, out_specs=out_specs, check_vma=False
    )
```

```python
import functools
import math

import jax
import jax.numpy as jnp
from jax import lax
from jax.experimental import pallas as pl
from jax.experimental.pallas import tpu as pltpu
from jax.sharding import PartitionSpec as P

BLOCK = 256
EPS = 1e-06
VMEM_LIMIT = 63 * 1024 * 1024
MESH = pl.DeviceIdType.MESH
F32 = jnp.float32
BF16 = jnp.bfloat16


def whole(count):
    return [pl.BlockSpec(memory_space=pltpu.VMEM)] * count


def dot_nn(a, b):
    return lax.dot_general(a, b, (((1,), (0,)), ((), ())), preferred_element_type=F32)


def dot_nt(a, b):
    return lax.dot_general(a, b, (((1,), (1,)), ((), ())), preferred_element_type=F32)


def dot_tn(a, b):
    return lax.dot_general(a, b, (((0,), (0,)), ((), ())), preferred_element_type=F32)


def params(**more):
    return pltpu.CompilerParams(vmem_limit_bytes=VMEM_LIMIT, **more)


def slot_row(groups, order, stride, cap_offset):
    size = groups.shape[1]
    groups_col = jnp.broadcast_to(groups, (size, size)).T
    order_col = jnp.broadcast_to(order, (size, size)).T
    earlier = (groups_col == groups) & (order_col < order)
    rank = jnp.sum(earlier.astype(F32), axis=0, keepdims=True).astype(jnp.int32)
    return groups * stride + rank + cap_offset


def one_hot_rows(slots, slot_count):
    size = slots.shape[1]
    ids = lax.broadcasted_iota(jnp.int32, (slot_count, size), 0)
    return jnp.where(ids == slots, 1.0, 0.0).astype(BF16)


def home_slots(places, tok_dev, stride, cap_offset):
    return slot_row(lax.div(places, jnp.int32(tok_dev)), places, stride, cap_offset)


def sorted_slots(order, tok_dev, stride, cap_offset):
    position = lax.broadcasted_iota(jnp.int32, order.shape, 1)
    return slot_row(lax.div(order, jnp.int32(tok_dev)), position, stride, cap_offset)


def dispatch_kernel(devices, capacity, chunk, places_ref, tokens_ref, cot_ref, *out_refs):
    rounds, tok_dev = places_ref.shape
    for hashing in range(rounds):
        places = places_ref[hashing : hashing + 1, :]
        slots = home_slots(places, tok_dev, chunk, 0)
        rows = dot_nn(one_hot_rows(slots, devices * chunk), tokens_ref[...])
        rows += dot_nn(one_hot_rows(slots + capacity, devices * chunk), cot_ref[...])
        out_refs[hashing][...] = rows.astype(BF16)


def normal_of(x, gain):
    return (x * lax.rsqrt(jnp.mean(x * x, axis=-1, keepdims=True) + EPS) * gain).astype(BF16)


def unit_of(q):
    depth = q.shape[-1]
    scale = lax.rsqrt(jnp.mean(q * q, axis=-1, keepdims=True) + EPS)
    return (q * scale / math.sqrt(depth)).astype(BF16)


def flipped(index, mask):
    bit = 1
    while bit <= mask:
        if mask & bit:
            index = index + bit * (1 - 2 * lax.rem(lax.div(index, bit), 2))
        bit *= 2
    return index


def forwarding_order(masks):
    return sorted(masks, key=lambda m: int(bin(m)[:1:-1].ljust(16, "0"), 2), reverse=True)


def core_kernel(heads, capacity, chunk, back_chunk, ahead, grad_scale, *refs):
    rounds = refs[0].shape[0]
    order_ref, gain_ref, qk_ref, v_ref, sums_ref, places_ref, tokens_ref = refs[:7]
    outgoing = refs[7 : 7 + rounds]
    d_tokens_ref, d_gain_ref, d_qk_ref, d_v_ref = refs[7 + rounds : 11 + rounds]
    (
        arrived, sorted_x, sorted_g, halo_x, normal, query, value, halo_q, halo_v,
        d_query, d_key, d_value, back_out, back_in, query_low, value_low, total,
        rows_out, rows_back, gain_out, gain_back, weights, sums_in, sums_run,
        send_sem, recv_sem, own_sem, halo_sem, back_sem, rows_sem, gain_sem, home_sem, sums_sem,
    ) = refs[11 + rounds :]
    devices = lax.axis_size("tok")
    me = lax.axis_index("tok")
    right, left = lax.rem(me + 1, devices), lax.rem(me + devices - 1, devices)
    rows, width = sorted_x.shape[1:]
    depth = width // heads
    slot_count = devices * chunk
    parts = [slice(head * depth, (head + 1) * depth) for head in range(heads)]

    barrier = pltpu.get_barrier_semaphore()
    for step in range(1, devices):
        peer = lax.rem(me + step, devices)
        pl.semaphore_signal(barrier, inc=1, device_id={"tok": peer}, device_id_type=MESH)
    own = [
        pltpu.make_async_copy(outgoing[r].at[me], arrived.at[r, me], own_sem.at[r])
        for r in range(rounds)
    ]
    for copy in own:
        copy.start()
    pl.semaphore_wait(barrier, devices - 1)

    def piece(r, step):
        peer = lax.rem(me + step, devices)
        return pltpu.make_async_remote_copy(
            src_ref=outgoing[r].at[peer],
            dst_ref=arrived.at[r, me],
            send_sem=send_sem.at[r, step - 1],
            recv_sem=recv_sem.at[r, step - 1],
            device_id={"tok": peer},
            device_id_type=MESH,
        )

    pieces = [[piece(r, step) for step in range(1, devices)] for r in range(rounds)]
    halos = [
        pltpu.make_async_remote_copy(
            src_ref=sorted_x.at[r],
            dst_ref=halo_x.at[r],
            send_sem=halo_sem.at[0, r],
            recv_sem=halo_sem.at[1, r],
            device_id={"tok": right},
            device_id_type=MESH,
        )
        for r in range(rounds)
    ]
    backs = [
        pltpu.make_async_remote_copy(
            src_ref=back_out.at[r],
            dst_ref=back_in.at[r],
            send_sem=back_sem.at[0, r],
            recv_sem=back_sem.at[1, r],
            device_id={"tok": left},
            device_id_type=MESH,
        )
        for r in range(rounds)
    ]


    def to_all(source, target, sems):
        copies = []
        for step in range(1, devices):
            peer = lax.rem(me + step, devices)
            copies.append(
                pltpu.make_async_remote_copy(
                    src_ref=source.at[peer],
                    dst_ref=target.at[me],
                    send_sem=sems.at[0, step - 1],
                    recv_sem=sems.at[1, step - 1],
                    device_id={"tok": peer},
                    device_id_type=MESH,
                )
            )
        return copies

    homeward = [to_all(rows_out.at[r], rows_back.at[r], rows_sem.at[r]) for r in range(rounds)]
    homeward.append(to_all(gain_out, gain_back, gain_sem))
    stay = [
        pltpu.make_async_copy(rows_out.at[r, me], rows_back.at[r, me], home_sem.at[r])
        for r in range(rounds)
    ]
    stay.append(pltpu.make_async_copy(gain_out.at[me], gain_back.at[me], home_sem.at[rounds]))

    def send_home(r):
        for copy in [*homeward[r], stay[r]]:
            copy.start()

    bits = devices.bit_length() - 1
    first_slot = [devices - (devices >> k) for k in range(bits)]

    def sums_copy(k, mask):
        slot = first_slot[k] + (mask >> (k + 1))
        source = weights.at[flipped(me, mask)] if k == 0 else sums_run.at[mask >> 1]
        return pltpu.make_async_remote_copy(
            src_ref=source,
            dst_ref=sums_in.at[slot],
            send_sem=sums_sem.at[0, slot],
            recv_sem=sums_sem.at[1, slot],
            device_id={"tok": flipped(me, 1 << k)},
            device_id_type=MESH,
        )

    stages = [
        {m: sums_copy(k, m) for m in range(1 << k, devices, 2 << k)} for k in range(bits)
    ]
    for copy in pieces[0]:
        copy.start()

    def sort(r):
        slots = sorted_slots(order_ref[r], rows, chunk, 0)
        data = arrived[r].reshape(slot_count, width)
        sorted_x[r] = dot_tn(one_hot_rows(slots, slot_count), data).astype(BF16)
        sorted_g[r] = dot_tn(one_hot_rows(slots + capacity, slot_count), data).astype(BF16)

    def project(r):
        normal[r] = normal_of(sorted_x[r].astype(F32), gain_ref[...])
        query[r] = dot_nn(normal[r], qk_ref[...]).astype(BF16)
        value[r] = dot_nn(normal[r], v_ref[...]).astype(BF16)

    def attend(r):
        behind = normal_of(halo_x[r].astype(F32), gain_ref[...])
        halo_q[...] = dot_nn(behind, qk_ref[...]).astype(BF16)
        halo_v[...] = dot_nn(behind, v_ref[...]).astype(BF16)
        sums = sums_ref[r].T
        diagonal = lax.broadcasted_iota(jnp.int32, (rows, rows), 0) == lax.broadcasted_iota(
            jnp.int32, (rows, rows), 1
        )
        for head, part in enumerate(parts):
            q = query[r, :, part]
            g = sorted_g[r, :, part]
            log_sum = sums[:, head : head + 1]
            keys = [unit_of(halo_q[:, part].astype(F32)), unit_of(q.astype(F32))]
            values = [halo_v[:, part], value[r, :, part]]
            weights = [jnp.exp(dot_nt(q, k) - log_sum) for k in keys]
            weights[1] = jnp.where(diagonal, 0.0, weights[1])
            d_weights = [dot_nt(g, v) for v in values]
            delta = jnp.sum(
                weights[0] * d_weights[0] + weights[1] * d_weights[1], -1, keepdims=True
            )
            d_scores = [(w * (d - delta)).astype(BF16) for w, d in zip(weights, d_weights)]
            low = [w.astype(BF16) for w in weights]
            back_out[r, :, part] = dot_tn(d_scores[0], q).astype(BF16)
            back_out[r, :, slice(width + part.start, width + part.stop)] = dot_tn(
                low[0], g
            ).astype(BF16)
            d_query[r, :, part] = dot_nn(d_scores[0], keys[0]) + dot_nn(d_scores[1], keys[1])
            d_key[r, :, part] = dot_tn(d_scores[1], q)
            d_value[r, :, part] = dot_tn(low[1], g)

    def finish(r):
        for part in parts:
            q = query[r, :, part].astype(F32)
            dk = d_key[r, :, part] + back_in[r, :, part].astype(F32)
            scale = lax.rsqrt(jnp.mean(q * q, axis=-1, keepdims=True) + EPS)
            along = jnp.mean(q * dk, axis=-1, keepdims=True)
            pulled = (dk * scale - q * (scale * scale * scale * along)) / math.sqrt(depth)
            query_low[:, part] = (d_query[r, :, part] + pulled).astype(BF16)
        value_low[...] = (d_value[r] + back_in[r, :, width:].astype(F32)).astype(BF16)
        d_normal = dot_nt(query_low[...], qk_ref[...]) + dot_nt(value_low[...], v_ref[...])
        x = sorted_x[r].astype(F32)
        scaled = x * lax.rsqrt(jnp.mean(x * x, axis=-1, keepdims=True) + EPS)
        slots = sorted_slots(order_ref[r], rows, back_chunk, 0)
        placed = dot_nn(one_hot_rows(slots, devices * back_chunk), d_normal.astype(BF16))
        rows_out[r] = placed.astype(BF16).reshape(devices, back_chunk, width)
        gain = jnp.sum(d_normal * scaled, axis=0, keepdims=True)
        for low, columns in (
            (query_low, slice(0, width)),
            (value_low, slice(width, 2 * width)),
        ):
            grad = dot_tn(normal[r], low[...])
            if r > 0:
                grad += total[:, columns]
            if r < rounds - 1:
                total[:, columns] = grad
            else:
                grad = (grad * grad_scale).astype(BF16)
                weights[:, :, columns] = grad.reshape(devices, width // devices, width)
            if columns.start == 0:
                send_home(r)
        return gain

    def go_home():
        for copy in stay:
            copy.wait()
        for copies in homeward:
            for copy in copies:
                copy.wait_recv()
        d_normal = jnp.zeros((rows, width), F32)
        for r in range(rounds):
            slots = home_slots(places_ref[r : r + 1, :], rows, back_chunk, 0)
            data = rows_back[r].reshape(devices * back_chunk, width)
            d_normal += dot_tn(one_hot_rows(slots, devices * back_chunk), data)
        x = tokens_ref[...].astype(F32)
        scale = lax.rsqrt(jnp.mean(x * x, axis=-1, keepdims=True) + EPS)
        t = d_normal * gain_ref[...]
        along = jnp.mean(x * t, axis=-1, keepdims=True)
        d_tokens_ref[...] = (t * scale - x * (scale * scale * scale * along)).astype(BF16)
        d_gain_ref[...] = jnp.sum(gain_back[:, 0, :], axis=0, keepdims=True)

    for r in range(rounds):
        if r + 1 < rounds:
            for copy in pieces[r + 1][:ahead]:
                copy.start()
        own[r].wait()
        for copy in pieces[r]:
            copy.wait_recv()
        sort(r)
        halos[r].start()
        if r + 1 < rounds:
            for copy in pieces[r + 1][ahead:]:
                copy.start()
        project(r)
        halos[r].wait_recv()
        attend(r)
        backs[r].start()
    gain_total = jnp.zeros((1, width), F32)
    for r in range(rounds):
        backs[r].wait_recv()
        gain_total += finish(r)
    gain_total = gain_total * grad_scale
    share = width // devices
    gain_out[...] = jnp.zeros(gain_out.shape, F32)
    for device in range(devices):
        gain_out[device, 0:1, 0:share] = gain_total[:, device * share : (device + 1) * share]
    for mask in forwarding_order(stages[0]):
        stages[0][mask].start()
    send_home(rounds)
    for k in range(bits):
        waiting = None
        for mask in forwarding_order(stages[k]):
            mine = mask - (1 << k)
            stages[k][mask].wait_recv()
            arrived_sum = sums_in[first_slot[k] + (mask >> (k + 1))].astype(F32)
            before = weights[flipped(me, mine)] if k == 0 else sums_run[mine >> 1]
            run = before.astype(F32) + arrived_sum
            if k == bits - 1:
                d_qk_ref[...] = run[:, :width]
                d_v_ref[...] = run[:, width:]
                continue
            sums_run[mine >> 1] = run.astype(BF16)
            if waiting is not None:
                waiting.start()
            waiting = stages[k + 1].get(mine)
        if waiting is not None:
            waiting.start()
        if k == min(1, bits - 1):
            go_home()
    for stage in stages:
        for copy in stage.values():
            copy.wait_send()
    for copies in homeward:
        for copy in copies:
            copy.wait_send()
    for r in range(rounds):
        for copy in pieces[r]:
            copy.wait_send()
        halos[r].wait_send()
        backs[r].wait_send()


def per_device(tokens, norm_gain, w_qk, w_v, cotangent, log_sums, bucket_order, token_position):
    devices = lax.axis_size("tok")
    me = lax.axis_index("tok")
    tok_dev, width = tokens.shape
    rounds, seq_len = bucket_order.shape
    heads = log_sums.shape[1]
    assert tok_dev == BLOCK
    capacity = 5 * tok_dev // (4 * devices)
    chunk = -(-2 * capacity // 8) * 8
    back_chunk = -(-capacity // 8) * 8
    slots = devices * chunk
    grad_scale = 1.0 / math.sqrt(seq_len)
    gain_row = norm_gain.reshape(1, width)
    my_order = lax.dynamic_slice_in_dim(bucket_order, me * tok_dev, tok_dev, axis=1).reshape(
        rounds, 1, tok_dev
    )
    outgoing = pl.pallas_call(
        functools.partial(dispatch_kernel, devices, capacity, chunk),
        out_shape=[jax.ShapeDtypeStruct((slots, width), BF16)] * rounds,
        in_specs=whole(3),
        out_specs=whole(rounds),
        compiler_params=params(),
        name="dispatch",
    )(token_position, tokens, cotangent)

    def low(*shape):
        return pltpu.VMEM(shape, BF16)

    per_round = (rounds, tok_dev, width)
    share = width // devices
    d_tokens, d_gain, d_qk, d_v = pl.pallas_call(
        functools.partial(
            core_kernel, heads, capacity, chunk, back_chunk, devices // 3, grad_scale
        ),
        out_shape=[
            jax.ShapeDtypeStruct((tok_dev, width), BF16),
            jax.ShapeDtypeStruct((1, 128), F32),
            jax.ShapeDtypeStruct((share, width), F32),
            jax.ShapeDtypeStruct((share, width), F32),
        ],
        in_specs=whole(7) + [pl.BlockSpec(memory_space=pl.ANY)] * rounds,
        out_specs=whole(4),
        scratch_shapes=[
            low(rounds, devices, chunk, width),
            *[low(*per_round)] * 6,
            *[low(tok_dev, width)] * 2,
            *[pltpu.VMEM(per_round, F32)] * 3,
            *[low(rounds, tok_dev, 2 * width)] * 2,
            *[low(tok_dev, width)] * 2,
            pltpu.VMEM((width, 2 * width), F32),
            *[low(rounds, devices, back_chunk, width)] * 2,
            *[pltpu.VMEM((devices, 8, 128), F32)] * 2,
            low(devices, share, 2 * width),
            low(devices - 1, share, 2 * width),
            low(devices // 2, share, 2 * width),
            pltpu.SemaphoreType.DMA((rounds, devices - 1)),
            pltpu.SemaphoreType.DMA((rounds, devices - 1)),
            pltpu.SemaphoreType.DMA((rounds,)),
            pltpu.SemaphoreType.DMA((2, rounds)),
            pltpu.SemaphoreType.DMA((2, rounds)),
            pltpu.SemaphoreType.DMA((rounds, 2, devices - 1)),
            pltpu.SemaphoreType.DMA((2, devices - 1)),
            pltpu.SemaphoreType.DMA((rounds + 1,)),
            pltpu.SemaphoreType.DMA((2, devices - 1)),
        ],
        compiler_params=params(collective_id=0, has_side_effects=True),
        name="core",
    )(
        my_order, gain_row, w_qk, w_v, log_sums, token_position, tokens,
        *[rows.reshape(devices, chunk, width) for rows in outgoing],
    )
    return (d_tokens, d_gain[0, :share], d_qk, d_v)


def solution(mesh):
    in_specs = (
        P(("groups", "tok"), None),
        P(),
        P(),
        P(),
        P(("groups", "tok"), None),
        P(None, None, ("groups", "tok")),
        P(None, "groups"),
        P(None, ("groups", "tok")),
    )
    out_specs = (
        P(("groups", "tok"), None),
        P(("groups", "tok")),
        P(("groups", "tok"), None),
        P(("groups", "tok"), None),
    )
    return jax.shard_map(
        per_device, mesh=mesh, in_specs=in_specs, out_specs=out_specs, check_vma=False
    )
```

```python
import functools
import math

import jax
import jax.numpy as jnp
from jax import lax
from jax.experimental import pallas as pl
from jax.experimental.pallas import tpu as pltpu
from jax.sharding import PartitionSpec as P

BLOCK = 256
EPS = 1e-06
VMEM_LIMIT = 63 * 1024 * 1024
MESH = pl.DeviceIdType.MESH
F32 = jnp.float32
BF16 = jnp.bfloat16


def whole(count):
    return [pl.BlockSpec(memory_space=pltpu.VMEM)] * count


def dot_nn(a, b):
    return lax.dot_general(a, b, (((1,), (0,)), ((), ())), preferred_element_type=F32)


def dot_nt(a, b):
    return lax.dot_general(a, b, (((1,), (1,)), ((), ())), preferred_element_type=F32)


def dot_tn(a, b):
    return lax.dot_general(a, b, (((0,), (0,)), ((), ())), preferred_element_type=F32)


def params(**more):
    return pltpu.CompilerParams(vmem_limit_bytes=VMEM_LIMIT, **more)


def slot_row(groups, order, stride, cap_offset):
    size = groups.shape[1]
    groups_col = jnp.broadcast_to(groups, (size, size)).T
    order_col = jnp.broadcast_to(order, (size, size)).T
    earlier = (groups_col == groups) & (order_col < order)
    rank = jnp.sum(earlier.astype(F32), axis=0, keepdims=True).astype(jnp.int32)
    return groups * stride + rank + cap_offset


def one_hot_rows(slots, slot_count):
    size = slots.shape[1]
    ids = lax.broadcasted_iota(jnp.int32, (slot_count, size), 0)
    return jnp.where(ids == slots, 1.0, 0.0).astype(BF16)


def home_slots(places, tok_dev, stride, cap_offset):
    return slot_row(lax.div(places, jnp.int32(tok_dev)), places, stride, cap_offset)


def sorted_slots(order, tok_dev, stride, cap_offset):
    position = lax.broadcasted_iota(jnp.int32, order.shape, 1)
    return slot_row(lax.div(order, jnp.int32(tok_dev)), position, stride, cap_offset)


def dispatch_kernel(devices, capacity, chunk, places_ref, tokens_ref, cot_ref, *out_refs):
    rounds, tok_dev = places_ref.shape
    for hashing in range(rounds):
        places = places_ref[hashing : hashing + 1, :]
        slots = home_slots(places, tok_dev, chunk, 0)
        rows = dot_nn(one_hot_rows(slots, devices * chunk), tokens_ref[...])
        rows += dot_nn(one_hot_rows(slots + capacity, devices * chunk), cot_ref[...])
        out_refs[hashing][...] = rows.astype(BF16)


def normal_of(x, gain):
    return (x * lax.rsqrt(jnp.mean(x * x, axis=-1, keepdims=True) + EPS) * gain).astype(BF16)


def unit_of(q):
    depth = q.shape[-1]
    scale = lax.rsqrt(jnp.mean(q * q, axis=-1, keepdims=True) + EPS)
    return (q * scale / math.sqrt(depth)).astype(BF16)


def flipped(index, mask):
    bit = 1
    while bit <= mask:
        if mask & bit:
            index = index + bit * (1 - 2 * lax.rem(lax.div(index, bit), 2))
        bit *= 2
    return index


def forwarding_order(masks):
    return sorted(masks, key=lambda m: int(bin(m)[:1:-1].ljust(16, "0"), 2), reverse=True)


def core_kernel(heads, capacity, chunk, back_chunk, ahead, grad_scale, *refs):
    rounds = refs[0].shape[0]
    order_ref, gain_ref, qk_ref, v_ref, sums_ref, places_ref, tokens_ref = refs[:7]
    outgoing = refs[7 : 7 + rounds]
    d_tokens_ref, d_gain_ref, d_weights_ref = refs[7 + rounds : 10 + rounds]
    (
        arrived, sorted_x, sorted_g, halo_x, normal, query, value, halo_q, halo_v,
        d_query, d_key, d_value, back_out, back_in, query_low, value_low, total,
        rows_out, rows_back, gain_out, gain_back, weights, sums_in, sums_run,
        send_sem, recv_sem, own_sem, halo_sem, back_sem, rows_sem, gain_sem, home_sem, sums_sem,
    ) = refs[10 + rounds :]
    devices = lax.axis_size("tok")
    me = lax.axis_index("tok")
    right, left = lax.rem(me + 1, devices), lax.rem(me + devices - 1, devices)
    rows, width = sorted_x.shape[1:]
    depth = width // heads
    slot_count = devices * chunk
    parts = [slice(head * depth, (head + 1) * depth) for head in range(heads)]

    barrier = pltpu.get_barrier_semaphore()
    for step in range(1, devices):
        peer = lax.rem(me + step, devices)
        pl.semaphore_signal(barrier, inc=1, device_id={"tok": peer}, device_id_type=MESH)
    own = [
        pltpu.make_async_copy(outgoing[r].at[me], arrived.at[r, me], own_sem.at[r])
        for r in range(rounds)
    ]
    for copy in own:
        copy.start()
    pl.semaphore_wait(barrier, devices - 1)

    def piece(r, step):
        peer = lax.rem(me + step, devices)
        return pltpu.make_async_remote_copy(
            src_ref=outgoing[r].at[peer],
            dst_ref=arrived.at[r, me],
            send_sem=send_sem.at[r, step - 1],
            recv_sem=recv_sem.at[r, step - 1],
            device_id={"tok": peer},
            device_id_type=MESH,
        )

    pieces = [[piece(r, step) for step in range(1, devices)] for r in range(rounds)]
    halos = [
        pltpu.make_async_remote_copy(
            src_ref=sorted_x.at[r],
            dst_ref=halo_x.at[r],
            send_sem=halo_sem.at[0, r],
            recv_sem=halo_sem.at[1, r],
            device_id={"tok": right},
            device_id_type=MESH,
        )
        for r in range(rounds)
    ]
    backs = [
        pltpu.make_async_remote_copy(
            src_ref=back_out.at[r],
            dst_ref=back_in.at[r],
            send_sem=back_sem.at[0, r],
            recv_sem=back_sem.at[1, r],
            device_id={"tok": left},
            device_id_type=MESH,
        )
        for r in range(rounds)
    ]


    def to_all(source, target, sems):
        copies = []
        for step in range(1, devices):
            peer = lax.rem(me + step, devices)
            copies.append(
                pltpu.make_async_remote_copy(
                    src_ref=source.at[peer],
                    dst_ref=target.at[me],
                    send_sem=sems.at[0, step - 1],
                    recv_sem=sems.at[1, step - 1],
                    device_id={"tok": peer},
                    device_id_type=MESH,
                )
            )
        return copies

    homeward = [to_all(rows_out.at[r], rows_back.at[r], rows_sem.at[r]) for r in range(rounds)]
    homeward.append(to_all(gain_out, gain_back, gain_sem))
    stay = [
        pltpu.make_async_copy(rows_out.at[r, me], rows_back.at[r, me], home_sem.at[r])
        for r in range(rounds)
    ]
    stay.append(pltpu.make_async_copy(gain_out.at[me], gain_back.at[me], home_sem.at[rounds]))

    def send_home(r):
        for copy in [*homeward[r], stay[r]]:
            copy.start()

    bits = devices.bit_length() - 1
    first_slot = [devices - (devices >> k) for k in range(bits)]

    def sums_copy(half, k, mask):
        slot = first_slot[k] + (mask >> (k + 1))
        source = weights.at[half, flipped(me, mask)] if k == 0 else sums_run.at[half, mask >> 1]
        return pltpu.make_async_remote_copy(
            src_ref=source,
            dst_ref=sums_in.at[half, slot],
            send_sem=sums_sem.at[half, 0, slot],
            recv_sem=sums_sem.at[half, 1, slot],
            device_id={"tok": flipped(me, 1 << k)},
            device_id_type=MESH,
        )

    stages = [
        [{m: sums_copy(half, k, m) for m in range(1 << k, devices, 2 << k)} for half in range(2)]
        for k in range(bits)
    ]
    for copy in pieces[0]:
        copy.start()

    def sort(r):
        slots = sorted_slots(order_ref[r], rows, chunk, 0)
        data = arrived[r].reshape(slot_count, width)
        sorted_x[r] = dot_tn(one_hot_rows(slots, slot_count), data).astype(BF16)
        sorted_g[r] = dot_tn(one_hot_rows(slots + capacity, slot_count), data).astype(BF16)

    def project(r):
        normal[r] = normal_of(sorted_x[r].astype(F32), gain_ref[...])
        query[r] = dot_nn(normal[r], qk_ref[...]).astype(BF16)
        value[r] = dot_nn(normal[r], v_ref[...]).astype(BF16)

    def attend(r):
        behind = normal_of(halo_x[r].astype(F32), gain_ref[...])
        halo_q[...] = dot_nn(behind, qk_ref[...]).astype(BF16)
        halo_v[...] = dot_nn(behind, v_ref[...]).astype(BF16)
        sums = sums_ref[r].T
        diagonal = lax.broadcasted_iota(jnp.int32, (rows, rows), 0) == lax.broadcasted_iota(
            jnp.int32, (rows, rows), 1
        )
        for head, part in enumerate(parts):
            q = query[r, :, part]
            g = sorted_g[r, :, part]
            log_sum = sums[:, head : head + 1]
            keys = [unit_of(halo_q[:, part].astype(F32)), unit_of(q.astype(F32))]
            values = [halo_v[:, part], value[r, :, part]]
            weights = [jnp.exp(dot_nt(q, k) - log_sum) for k in keys]
            weights[1] = jnp.where(diagonal, 0.0, weights[1])
            d_weights = [dot_nt(g, v) for v in values]
            delta = jnp.sum(
                weights[0] * d_weights[0] + weights[1] * d_weights[1], -1, keepdims=True
            )
            d_scores = [(w * (d - delta)).astype(BF16) for w, d in zip(weights, d_weights)]
            low = [w.astype(BF16) for w in weights]
            back_out[r, :, part] = dot_tn(d_scores[0], q).astype(BF16)
            back_out[r, :, slice(width + part.start, width + part.stop)] = dot_tn(
                low[0], g
            ).astype(BF16)
            d_query[r, :, part] = dot_nn(d_scores[0], keys[0]) + dot_nn(d_scores[1], keys[1])
            d_key[r, :, part] = dot_tn(d_scores[1], q)
            d_value[r, :, part] = dot_tn(low[1], g)

    def finish(r):
        for part in parts:
            q = query[r, :, part].astype(F32)
            dk = d_key[r, :, part] + back_in[r, :, part].astype(F32)
            scale = lax.rsqrt(jnp.mean(q * q, axis=-1, keepdims=True) + EPS)
            along = jnp.mean(q * dk, axis=-1, keepdims=True)
            pulled = (dk * scale - q * (scale * scale * scale * along)) / math.sqrt(depth)
            query_low[:, part] = (d_query[r, :, part] + pulled).astype(BF16)
        value_low[...] = (d_value[r] + back_in[r, :, width:].astype(F32)).astype(BF16)

        def row_gradients():
            d_normal = dot_nt(query_low[...], qk_ref[...]) + dot_nt(value_low[...], v_ref[...])
            x = sorted_x[r].astype(F32)
            scaled = x * lax.rsqrt(jnp.mean(x * x, axis=-1, keepdims=True) + EPS)
            slots = sorted_slots(order_ref[r], rows, back_chunk, 0)
            placed = dot_nn(one_hot_rows(slots, devices * back_chunk), d_normal.astype(BF16))
            rows_out[r] = placed.astype(BF16).reshape(devices, back_chunk, width)
            return jnp.sum(d_normal * scaled, axis=0, keepdims=True)

        def weight_gradients(half):
            columns = slice(half * width, (half + 1) * width)
            grad = dot_tn(normal[r], (query_low, value_low)[half][...])
            if r > 0:
                grad += total[:, columns]
            if r < rounds - 1:
                total[:, columns] = grad
            else:
                grad = (grad * grad_scale).astype(BF16)
                weights[half] = grad.reshape(devices, width // devices, width)

        if r < rounds - 1:
            gain = row_gradients()
            weight_gradients(0)
            send_home(r)
            weight_gradients(1)
        else:
            weight_gradients(0)
            weight_gradients(1)
            start_sums(0)
            gain = row_gradients()
            start_sums(1)
        return gain

    def start_sums(half):
        for mask in forwarding_order(stages[0][half]):
            stages[0][half][mask].start()

    def go_home():
        for copy in stay:
            copy.wait()
        for copies in homeward:
            for copy in copies:
                copy.wait_recv()
        d_normal = jnp.zeros((rows, width), F32)
        for r in range(rounds):
            slots = home_slots(places_ref[r : r + 1, :], rows, back_chunk, 0)
            data = rows_back[r].reshape(devices * back_chunk, width)
            d_normal += dot_tn(one_hot_rows(slots, devices * back_chunk), data)
        x = tokens_ref[...].astype(F32)
        scale = lax.rsqrt(jnp.mean(x * x, axis=-1, keepdims=True) + EPS)
        t = d_normal * gain_ref[...]
        along = jnp.mean(x * t, axis=-1, keepdims=True)
        d_tokens_ref[...] = (t * scale - x * (scale * scale * scale * along)).astype(BF16)
        d_gain_ref[...] = jnp.sum(gain_back[:, 0, :], axis=0, keepdims=True)

    for r in range(rounds):
        if r + 1 < rounds:
            for copy in pieces[r + 1][:ahead]:
                copy.start()
        own[r].wait()
        for copy in pieces[r]:
            copy.wait_recv()
        sort(r)
        halos[r].start()
        if r + 1 < rounds:
            for copy in pieces[r + 1][ahead:]:
                copy.start()
        project(r)
        halos[r].wait_recv()
        attend(r)
        backs[r].start()
    gain_total = jnp.zeros((1, width), F32)
    for r in range(rounds):
        backs[r].wait_recv()
        gain_total += finish(r)
    gain_total = gain_total * grad_scale
    share = width // devices
    gain_out[...] = jnp.zeros(gain_out.shape, F32)
    for device in range(devices):
        gain_out[device, 0:1, 0:share] = gain_total[:, device * share : (device + 1) * share]
    send_home(rounds - 1)
    send_home(rounds)
    for k in range(bits):
        waiting = None
        for half in range(2):
            for mask in forwarding_order(stages[k][half]):
                mine = mask - (1 << k)
                stages[k][half][mask].wait_recv()
                arrived_sum = sums_in[half, first_slot[k] + (mask >> (k + 1))].astype(F32)
                before = weights[half, flipped(me, mine)] if k == 0 else sums_run[half, mine >> 1]
                run = before.astype(F32) + arrived_sum
                if k == bits - 1:
                    d_weights_ref[:, half * width : (half + 1) * width] = run
                    continue
                sums_run[half, mine >> 1] = run.astype(BF16)
                if waiting is not None:
                    waiting.start()
                waiting = stages[k + 1][half].get(mine)
        if waiting is not None:
            waiting.start()
        if k == min(1, bits - 1):
            go_home()
    for stage in stages:
        for copy in [*stage[0].values(), *stage[1].values()]:
            copy.wait_send()
    for copies in homeward:
        for copy in copies:
            copy.wait_send()
    for r in range(rounds):
        for copy in pieces[r]:
            copy.wait_send()
        halos[r].wait_send()
        backs[r].wait_send()


def per_device(tokens, norm_gain, w_qk, w_v, cotangent, log_sums, bucket_order, token_position):
    devices = lax.axis_size("tok")
    me = lax.axis_index("tok")
    tok_dev, width = tokens.shape
    rounds, seq_len = bucket_order.shape
    heads = log_sums.shape[1]
    assert tok_dev == BLOCK
    capacity = 5 * tok_dev // (4 * devices)
    chunk = -(-2 * capacity // 8) * 8
    back_chunk = -(-capacity // 8) * 8
    slots = devices * chunk
    grad_scale = 1.0 / math.sqrt(seq_len)
    gain_row = norm_gain.reshape(1, width)
    my_order = lax.dynamic_slice_in_dim(bucket_order, me * tok_dev, tok_dev, axis=1).reshape(
        rounds, 1, tok_dev
    )
    outgoing = pl.pallas_call(
        functools.partial(dispatch_kernel, devices, capacity, chunk),
        out_shape=[jax.ShapeDtypeStruct((slots, width), BF16)] * rounds,
        in_specs=whole(3),
        out_specs=whole(rounds),
        compiler_params=params(),
        name="dispatch",
    )(token_position, tokens, cotangent)

    def low(*shape):
        return pltpu.VMEM(shape, BF16)

    per_round = (rounds, tok_dev, width)
    share = width // devices
    d_tokens, d_gain, d_weights = pl.pallas_call(
        functools.partial(
            core_kernel, heads, capacity, chunk, back_chunk, devices // 3, grad_scale
        ),
        out_shape=[
            jax.ShapeDtypeStruct((tok_dev, width), BF16),
            jax.ShapeDtypeStruct((1, 128), F32),
            jax.ShapeDtypeStruct((share, 2 * width), F32),
        ],
        in_specs=whole(7) + [pl.BlockSpec(memory_space=pl.ANY)] * rounds,
        out_specs=whole(3),
        scratch_shapes=[
            low(rounds, devices, chunk, width),
            *[low(*per_round)] * 6,
            *[low(tok_dev, width)] * 2,
            *[pltpu.VMEM(per_round, F32)] * 3,
            *[low(rounds, tok_dev, 2 * width)] * 2,
            *[low(tok_dev, width)] * 2,
            pltpu.VMEM((width, 2 * width), F32),
            *[low(rounds, devices, back_chunk, width)] * 2,
            *[pltpu.VMEM((devices, 8, 128), F32)] * 2,
            low(2, devices, share, width),
            low(2, devices - 1, share, width),
            low(2, devices // 2, share, width),
            pltpu.SemaphoreType.DMA((rounds, devices - 1)),
            pltpu.SemaphoreType.DMA((rounds, devices - 1)),
            pltpu.SemaphoreType.DMA((rounds,)),
            pltpu.SemaphoreType.DMA((2, rounds)),
            pltpu.SemaphoreType.DMA((2, rounds)),
            pltpu.SemaphoreType.DMA((rounds, 2, devices - 1)),
            pltpu.SemaphoreType.DMA((2, devices - 1)),
            pltpu.SemaphoreType.DMA((rounds + 1,)),
            pltpu.SemaphoreType.DMA((2, 2, devices - 1)),
        ],
        compiler_params=params(collective_id=0, has_side_effects=True),
        name="core",
    )(
        my_order, gain_row, w_qk, w_v, log_sums, token_position, tokens,
        *[rows.reshape(devices, chunk, width) for rows in outgoing],
    )
    return (d_tokens, d_gain[0, :share], d_weights[:, :width], d_weights[:, width:])


def solution(mesh):
    in_specs = (
        P(("groups", "tok"), None),
        P(),
        P(),
        P(),
        P(("groups", "tok"), None),
        P(None, None, ("groups", "tok")),
        P(None, "groups"),
        P(None, ("groups", "tok")),
    )
    out_specs = (
        P(("groups", "tok"), None),
        P(("groups", "tok")),
        P(("groups", "tok"), None),
        P(("groups", "tok"), None),
    )
    return jax.shard_map(
        per_device, mesh=mesh, in_specs=in_specs, out_specs=out_specs, check_vma=False
    )
```
